32 devices in a mesh: groups: 1, blk: 32 (over z, y, x, core).
Axes of the slice: x: 2, y: 2, z: 4, core: 2. Of those that a mesh axis runs over, the one named last changes fastest.
Arguments:
- queries: float32 [256, 24576], P('groups', 'blk'), may hold values from -8 to 8
- cache: float32 [2048, 576], P(('groups', 'blk')), may hold values from -8 to 8
- owner: int32 [2048], P(('groups', 'blk')), may hold values from 0 to 1, as said below
- prefix_len: int32 [2], P('groups'), may hold values from 1 to 1152, as said below
- key_up: float32 [128, 512, 128], P('blk'), may hold values from -0.25 to 0.25
- value_up: float32 [128, 512, 128], P('blk'), may hold values from -0.25 to 0.25
- out_weight: float32 [16384, 7168], P('blk'), may hold values from -0.5 to 0.5
Outputs:
- mixed: float32 [256, 7168], P(('groups', 'blk'))
The draws below stay inside these ranges and needn't reach their ends.
Inputs may be any that keep to these rules, and one draw needn't show every extreme that they name: `owner`: every request owns between 768 and 1280 slots, spread over the slots in no fixed order; some request owns exactly the fewest. prefix_len[r] + 128 is at most the number of slots that request r owns.
All inputs are finite; a program needn't handle non-finite values.
Results may differ from the reference program's by a relative error of at most 0.0003.
Values sent between devices are 32-bit elements; how exact they have to be, the bound alone decides.
No kernel may reach another device: no remote copies, remote signals or barrier semaphores. Data moves between devices by JAX's collectives and lax.ppermute only.
A program may use at most 64 MiB of HBM per device.

```python
import jax
import jax.numpy as jnp
from jax import lax

D = 7168
HEADS = 128
LATENT = 512
ROPE = 64
NOPE = 128
VDIM = 128
SPAN = 128
REQS = 2
ROWS = 256
CACHE = 2048


def plan_slots(key):
    base = jax.random.fold_in(key, 7301)
    first_key, second_key, third_key = jax.random.split(base, 3)
    chosen = jax.random.randint(jax.random.fold_in(base, 55), (), 0, REQS).astype(jnp.int32)
    req_ids = jnp.arange(REQS, dtype=jnp.int32)
    most_shift = CACHE // (4 * REQS)
    shifts = jax.random.randint(first_key, (REQS,), 0, most_shift + 1).astype(jnp.int32)
    shifts = jnp.where(req_ids == chosen, most_shift, jnp.where(req_ids == (chosen + 1) % REQS, 0, shifts)).astype(jnp.int32)
    counts = (CACHE // REQS + shifts - jnp.roll(shifts, 1)).astype(jnp.int32)
    ends = jnp.cumsum(counts)
    slot_ids = jnp.arange(CACHE, dtype=jnp.int32)
    ordered = jnp.sum((slot_ids[:, None] >= ends[None, :-1]).astype(jnp.int32), axis=1).astype(jnp.int32)
    shuffle = jax.random.permutation(second_key, CACHE)
    owners = ordered[shuffle]
    prefixes = jax.random.randint(third_key, (REQS,), 1, counts - SPAN + 1).astype(jnp.int32)
    prefixes = jnp.where(req_ids == chosen, counts - SPAN, prefixes).astype(jnp.int32)
    return (owners, prefixes)


def draw_owner(key, part):
    return plan_slots(key)[0]


def draw_prefix_len(key, part):
    return plan_slots(key)[1]


def draw_cache(key, part):
    base = jax.random.fold_in(key, 4409)
    lat_key, rope_key = jax.random.split(base)
    latent = jnp.clip(jax.random.normal(lat_key, (CACHE, LATENT), jnp.float32), -8.0, 8.0)
    rope = jnp.clip(jax.random.normal(rope_key, (CACHE, ROPE), jnp.float32), -8.0, 8.0)
    return jnp.concatenate([latent, rope], axis=1)


def draw_queries(key, part):
    width = NOPE + ROPE
    base = jax.random.fold_in(key, 6211)
    values = jnp.clip(1.5 * jax.random.normal(base, (ROWS, HEADS, width), jnp.float32), -8.0, 8.0)
    return values.reshape(ROWS, HEADS * width)


def level_of(own_key, shape, cuts, low, largest):
    def one(dim, parts):
        draws = jax.random.uniform(jax.random.fold_in(jax.random.fold_in(own_key, 6), dim), (parts,), jnp.float32, low / len(cuts), largest / len(cuts))
        return jnp.repeat(jnp.exp(draws), shape[dim] // parts).reshape((-1,) + (1,) * (len(shape) - dim - 1))

    factor_of = one(*cuts[0])
    for cut in cuts[1:]:
        factor_of = factor_of * one(*cut)
    return factor_of


def scatter_about(own_key, shape, deviation, limit, shards=(), kind=jnp.bfloat16):
    entries = jax.random.normal(own_key, shape, jnp.float32) * deviation
    if len(shards) > 0:
        entries = level_of(own_key, shape, shards, -0.22, 0.18) * entries
    return jnp.clip(entries, min=-limit, max=limit).astype(kind)


def setup_inputs(seed: int = 0, part: int = 0) -> dict:
    key_list = jax.random.split(jax.random.key(seed), 8)
    part_splits = jax.random.split(jax.random.fold_in(key_list[7], part), 8)
    queries = draw_queries(jax.random.fold_in(jax.random.fold_in(key_list[7], part), 71), part)
    cache = draw_cache(jax.random.fold_in(jax.random.fold_in(key_list[7], part), 71), part)
    owner = draw_owner(jax.random.fold_in(jax.random.fold_in(key_list[7], part), 71), part)
    prefix_len = draw_prefix_len(jax.random.fold_in(jax.random.fold_in(key_list[7], part), 71), part)
    key_up = scatter_about(key_list[4], (HEADS, LATENT, NOPE), LATENT ** -0.5, 0.25, ((0, 32),), jnp.float32)
    value_up = scatter_about(key_list[5], (HEADS, LATENT, VDIM), LATENT ** -0.5, 0.25, ((0, 32),), jnp.float32)
    out_weight = scatter_about(key_list[6], (HEADS * VDIM, D), VDIM ** -0.5, 0.5, ((0, 32),), jnp.float32)
    return {"queries": queries, "cache": cache, "owner": owner, "prefix_len": prefix_len, "key_up": key_up, "value_up": value_up, "out_weight": out_weight}


def reference(queries, cache, owner, prefix_len, key_up, value_up, out_weight):
    width = NOPE + ROPE
    hp = lax.Precision.HIGHEST
    q3 = queries.reshape(ROWS, HEADS, width)
    onehot = (owner[:, None] == jnp.arange(REQS, dtype=jnp.int32)[None, :]).astype(jnp.int32)
    position = lax.optimization_barrier(jnp.sum(onehot * (jnp.cumsum(onehot, axis=0) - 1), axis=1)).astype(jnp.int32)
    rel = (position - lax.optimization_barrier(jnp.sum(onehot * prefix_len[None, :], axis=1))).astype(jnp.int32)
    row_ids = jnp.arange(ROWS, dtype=jnp.int32)
    visible = (owner[None, :] == (row_ids // SPAN)[:, None]) & (rel[None, :] <= (row_ids % SPAN)[:, None])
    latent = cache[:, :LATENT]
    rope_keys = cache[:, LATENT:]
    scale = 1.0 / jnp.sqrt(jnp.float32(width))

    def one_head(items):
        q_head, k_up, v_up = items
        keys = jnp.dot(latent, k_up, precision=hp, preferred_element_type=jnp.float32)
        values = jnp.dot(latent, v_up, precision=hp, preferred_element_type=jnp.float32)
        score = jnp.dot(q_head[:, :NOPE], keys.T, precision=hp, preferred_element_type=jnp.float32)
        score = score + jnp.dot(q_head[:, NOPE:], rope_keys.T, precision=hp, preferred_element_type=jnp.float32)
        score = jnp.where(visible, score * scale, -jnp.inf)
        top = lax.optimization_barrier(jnp.max(score, axis=1, keepdims=True))
        expo = jnp.where(visible, jnp.exp(score - top), 0.0)
        weight = expo / lax.optimization_barrier(jnp.sum(expo, axis=1, keepdims=True))
        return jnp.dot(weight, values, precision=hp, preferred_element_type=jnp.float32)
    head_out = lax.map(one_head, (jnp.transpose(q3, (1, 0, 2)), key_up, value_up))
    flat = jnp.transpose(head_out, (1, 0, 2)).reshape(ROWS, HEADS * VDIM)
    return jnp.dot(flat, out_weight, precision=hp, preferred_element_type=jnp.float32)
```

```python
import math

import jax
import jax.numpy as jnp
from jax import lax
from jax.sharding import PartitionSpec as P

LATENT = 512
ROPE = 64
NOPE = 128
VDIM = 128
SPAN = 128
REQS = 2
PARTS = 3
HIGH = lax.Precision.HIGH


def orders_of(bits):
    middle = list(range(1, bits - 1))
    out = []
    for p in range(PARTS):
        turn = p % max(len(middle), 1)
        out.append([0] + middle[turn:] + middle[:turn] + ([bits - 1] if bits > 1 else []))
    return out


def cuts(total, unit, parts):
    units = total // unit
    edges = [(units * p) // parts * unit for p in range(parts)] + [total]
    return [(edges[p], edges[p + 1]) for p in range(parts)]


def swap(x, bit, size):
    return lax.ppermute(x, "blk", [(i, i ^ (1 << bit)) for i in range(size)])


def gather(block, size, order):
    bits = size.bit_length() - 1
    held = block[None]
    taken = []
    for bit in order:
        held = jnp.concatenate([held[None], swap(held, bit, size)[None]], axis=0)
        held = held.reshape((-1,) + block.shape)
        taken.append(bit)
    full = held.reshape((2,) * bits + block.shape)
    place = [taken[::-1].index(b) for b in range(bits - 1, -1, -1)]
    full = jnp.transpose(full, place + list(range(bits, full.ndim)))
    return full.reshape((size,) + block.shape)


def scatter_step(keep, got, axis):
    lo = lambda x: lax.index_in_dim(x, 0, axis, False)
    hi = lambda x: lax.index_in_dim(x, 1, axis, False)
    return hi(keep) + hi(got), lo(keep) + lo(got)


def scatter(partial, size, order):
    bits = size.bit_length() - 1
    left = list(range(bits - 1, -1, -1))
    full = partial.reshape((2,) * bits + partial.shape[1:])
    axis = left.index(order[0])
    send = lax.index_in_dim(full, 1, axis, False)
    keep = lax.index_in_dim(full, 0, axis, False)
    left.remove(order[0])
    for step, bit in enumerate(order):
        got = swap(send, bit, size)
        if step == len(order) - 1:
            return keep + got
        axis = left.index(order[step + 1])
        left.remove(order[step + 1])
        send, keep = scatter_step(keep, got, axis)


def on_device(size, queries, cache, owner, prefix_len, key_up, value_up, out_weight):
    bits = size.bit_length() - 1
    width = NOPE + ROPE
    heads_dev = key_up.shape[0]
    rows_all = queries.shape[0]
    rows_dev = rows_all // size
    slots = cache.shape[0]
    scale = 1.0 / math.sqrt(width)
    me = lax.axis_index("blk")
    rel = jnp.arange(size, dtype=jnp.int32) ^ me

    req_ids = jnp.arange(REQS, dtype=jnp.int32)
    onehot = (owner[:, None] == req_ids[None, :]).astype(jnp.int32)
    earlier = jnp.tril(jnp.ones((slots, slots), jnp.int32), -1)
    before = jnp.sum(earlier[:, :, None] * onehot[None, :, :], axis=1)
    rank = jnp.sum(onehot * before, axis=1)
    count = jnp.sum(onehot, axis=0)
    tail = jnp.concatenate(
        [owner[:, None], rank[:, None], jnp.broadcast_to(count[None, :], (slots, REQS))], axis=1
    ).astype(jnp.float32)
    packed = jnp.concatenate([cache, tail], axis=1)
    orders = [o[::-1] for o in orders_of(bits)]
    pieces = [
        gather(packed[a:b], size, o) for (a, b), o in zip(cuts(slots, 8, PARTS), orders)
    ]
    slab = jnp.concatenate(pieces, axis=1)

    q3 = queries.reshape(size, rows_dev, heads_dev * width)[rel].reshape(rows_all, heads_dev, width) * scale
    q_latent = jnp.einsum("rhn,hln->rhl", q3[:, :, :NOPE], key_up, precision=HIGH, preferred_element_type=jnp.float32)
    counts_all = slab[:, 0, LATENT + ROPE + 2 :].astype(jnp.int32)
    base = jnp.sum((rel[None, :] < rel[:, None]).astype(jnp.int32)[:, :, None] * counts_all[None], axis=1)
    owners = slab[:, :, LATENT + ROPE].astype(jnp.int32)
    ranks = slab[:, :, LATENT + ROPE + 1].astype(jnp.int32)
    hot = (owners[:, :, None] == req_ids).astype(jnp.int32)
    reach = ranks + jnp.sum(hot * (base[:, None, :] - prefix_len[None, None, :]), axis=2)
    reach = reach.reshape(-1)
    owners = owners.reshape(-1)
    rows = (rel[:, None] * rows_dev + jnp.arange(rows_dev, dtype=jnp.int32)[None]).reshape(-1)
    visible = (owners[None, :] == (rows // SPAN)[:, None]) & (reach[None, :] <= (rows % SPAN)[:, None])
    flat = slab.reshape(size * slots, -1)
    latent = flat[:, :LATENT]
    score = jnp.einsum("rhl,tl->rht", q_latent, latent, precision=HIGH, preferred_element_type=jnp.float32)
    score = score + jnp.einsum("rhe,te->rht", q3[:, :, NOPE:], flat[:, LATENT : LATENT + ROPE], precision=HIGH, preferred_element_type=jnp.float32)
    masked = jnp.where(visible[:, None, :], score, -1e30)
    top = jnp.max(masked, axis=2)
    expo = jnp.where(visible[:, None, :], jnp.exp(score - top[:, :, None]), 0.0)
    total = jnp.sum(expo, axis=2)
    acc = jnp.einsum("rht,tl->rhl", expo, latent, precision=HIGH, preferred_element_type=jnp.float32)
    averaged = acc / total[:, :, None]
    head_out = jnp.einsum("rhl,hlv->rhv", averaged, value_up, precision=HIGH, preferred_element_type=jnp.float32)
    flat_out = head_out.reshape(rows_all, heads_dev * VDIM)
    outs = []
    for (a, b), o in zip(cuts(out_weight.shape[1], 128, PARTS), orders_of(bits)):
        partial = jnp.dot(flat_out, out_weight[:, a:b], precision=HIGH, preferred_element_type=jnp.float32)
        outs.append(scatter(partial.reshape(size, rows_dev, b - a), size, o))
    return jnp.concatenate(outs, axis=1)


def solution(mesh):
    placed = (
        P("groups", "blk"),
        P(("groups", "blk"), None),
        P(("groups", "blk")),
        P("groups"),
        P("blk", None, None),
        P("blk", None, None),
        P("blk", None),
    )
    size = mesh.shape["blk"]

    def step(*args):
        return on_device(size, *args)

    return jax.shard_map(
        step, mesh=mesh, in_specs=placed, out_specs=P(("groups", "blk"), None), check_vma=False
    )
```

```python
import functools
import math

import jax
import jax.numpy as jnp
from jax import lax
from jax.experimental import pallas as pl
from jax.experimental.pallas import tpu as pltpu
from jax.sharding import PartitionSpec as P


LATENT = 512
ROPE = 64
NOPE = 128
VDIM = 128
SPAN = 128
REQS = 2
PARTS = 3
LANES = 128
PACKED = LATENT + LANES
BLOCK = 512
FAR = 1e9
LOW = -1e30
FLOOR = -1e29
TILE = 256
PAIR = 2
F32 = jnp.float32
BF16 = jnp.bfloat16


def orders_of(bits):
    middle = list(range(1, bits - 1))
    out = []
    for p in range(PARTS):
        turn = p % max(len(middle), 1)
        out.append([0] + middle[turn:] + middle[:turn] + [bits - 1])
    return out


def cuts(total, unit):
    units = total // unit
    edges = [-(-units * p // PARTS) * unit for p in range(PARTS)] + [total]
    return [(edges[p], edges[p + 1]) for p in range(PARTS)]


def swap(x, bit, size):
    return lax.ppermute(x, "blk", [(i, i ^ (1 << bit)) for i in range(size)])


def split(x):
    hi = x.astype(BF16)
    return hi, (x - hi.astype(F32)).astype(BF16)


def pack_kernel(cache_ref, owner_ref, out_ref, count_ref):
    slots = cache_ref.shape[0]
    row = lax.broadcasted_iota(jnp.int32, (slots, slots), 0)
    col = lax.broadcasted_iota(jnp.int32, (slots, slots), 1)
    who = jnp.broadcast_to(owner_ref[...].astype(F32), (slots, slots))
    mine = jnp.sum(jnp.where(row == col, who, 0.0), axis=1, keepdims=True)
    ones = jnp.sum(jnp.where(col < row, who, 0.0), axis=1, keepdims=True)
    place = lax.broadcasted_iota(jnp.int32, (slots, 1), 0).astype(F32)
    rank = jnp.where(mine == 1.0, ones, place - ones)
    out_ref[:, :LATENT] = cache_ref[:, :LATENT]
    out_ref[:, LATENT : LATENT + ROPE] = cache_ref[:, LATENT:]
    lane = lax.broadcasted_iota(jnp.int32, (slots, LANES - ROPE), 1)
    out_ref[:, LATENT + ROPE :] = jnp.where(lane == 0, mine, jnp.where(lane == 1, rank, 0.0))
    total = jnp.sum(owner_ref[...].astype(F32), axis=1, keepdims=True)
    which = lax.broadcasted_iota(jnp.int32, count_ref.shape, 0)
    count_ref[...] = jnp.where(which == 0, slots - total, total)


def pack(cache, owner):
    slots = cache.shape[0]
    return pl.pallas_call(
        pack_kernel,
        out_shape=(
            jax.ShapeDtypeStruct((slots, PACKED), F32),
            jax.ShapeDtypeStruct((8, LANES), F32),
        ),
        name="pack",
    )(cache, owner.reshape(1, slots))


def query_kernel(size, me_ref, q_ref, out_ref):
    heads = out_ref.shape[0]
    rows_dev = q_ref.shape[1]
    bits = size.bit_length() - 1
    width = NOPE + ROPE
    blank = jnp.zeros((rows_dev, 2 * NOPE - width), F32)
    for place in range(size):
        rel = ((place & (size // 2 - 1)) << 1) | (place >> (bits - 1))
        x = q_ref[rel ^ me_ref[0]] * (1.0 / math.sqrt(width))
        rows = slice(place * rows_dev, (place + 1) * rows_dev)
        for h in range(heads):
            at = h * width
            out_ref[h, rows, :NOPE] = x[:, at : at + NOPE]
            out_ref[h, rows, NOPE:] = jnp.concatenate([x[:, at + NOPE : at + width], blank], axis=1)


def arrange(size, me, queries, heads):
    rows_all, cols = queries.shape
    return pl.pallas_call(
        functools.partial(query_kernel, size),
        out_shape=jax.ShapeDtypeStruct((heads, rows_all, 2 * NOPE), F32),
        grid_spec=pltpu.PrefetchScalarGridSpec(
            num_scalar_prefetch=1,
            grid=(1,),
            in_specs=[pl.BlockSpec((size, rows_all // size, cols), lambda i, *_: (0, 0, 0))],
            out_specs=pl.BlockSpec((heads, rows_all, 2 * NOPE), lambda i, *_: (0, 0, 0)),
        ),
        cost_estimate=pl.CostEstimate(flops=0, bytes_accessed=8 * rows_all * cols, transcendentals=0),
        name="arrange",
    )(me, queries.reshape(size, rows_all // size, cols))


def stack3(x, axis, low):
    hi, lo = x
    return jnp.concatenate([hi, lo, hi] if low else [hi, hi, lo], axis=axis)


def attend_kernel(size, places, last, me_ref, prefix_ref, count_ref, *refs):
    n = 2 * PARTS
    pieces = refs[:n]
    q_ref, ku_ref, vu_ref = refs[n : n + 3]
    refs = refs[n + 3 :]
    if last:
        m_in, l_in, acc_in, hi_out, lo_out = refs[:5]
        refs = refs[5:]
    else:
        m_out, l_out, acc_out = refs[:3]
        refs = refs[3:]
    lat_hi, lat_lo, rope_hi, rope_lo, key_hi, key_lo, val_t, reach_ref, score_ref, expo_hi, expo_lo = refs
    rows_all = q_ref.shape[1]
    slots = lat_hi.shape[0]
    me = me_ref[0]
    bits = size.bit_length() - 1
    mul = lambda x, y, c: lax.dot_general(x, y, (c, ((), ())), preferred_element_type=F32)
    plain = ((1,), (0,))
    half = LANES // REQS

    @pl.when(pl.program_id(0) == 0)
    def _():
        at = 0
        for ref in pieces:
            m, s, _ = ref.shape
            for j in range(0, m, 2):
                x = ref[j : j + 2].reshape(2 * s, PACKED)
                hi, lo = split(x)
                rows = slice(at + j * s, at + (j + 2) * s)
                lat_hi[rows, :] = hi[:, :LATENT]
                lat_lo[rows, :] = lo[:, :LATENT]
                rope_hi[rows, :] = hi[:, LATENT:]
                rope_lo[rows, :] = lo[:, LATENT:]
            at += m * s
        row = lax.broadcasted_iota(jnp.int32, (LANES, 2 * LANES), 0)
        col = lax.broadcasted_iota(jnp.int32, (LANES, 2 * LANES), 1)
        pick = jnp.where(row == ROPE + col // LANES, 1.0, 0.0).astype(BF16)
        told = mul(rope_hi[...], pick, plain)
        lane = lax.broadcasted_iota(jnp.int32, (1, LANES), 1)
        want = ((lane // half) ^ (me >> (bits - 1))).astype(F32)
        index = lax.broadcasted_iota(jnp.int32, (size, LANES), 0)
        device = index ^ me
        counts = jnp.where(want == 0.0, count_ref[:, 0, :], count_ref[:, 1, :])
        ahead = jnp.where(want == 0.0, prefix_ref[0].astype(F32), prefix_ref[1].astype(F32))
        at = 0
        for ref, where in zip(pieces, places):
            m, s, _ = ref.shape
            for j, r in enumerate(where):
                before = jnp.where(device < (me ^ r), counts, 0.0)
                base = jnp.sum(before, axis=0, keepdims=True) - ahead
                rows = slice(at + j * s, at + (j + 1) * s)
                here = told[rows, LANES:] + base
                reach_ref[rows, :] = jnp.where(told[rows, :LANES] == want, here, FAR)
            at += m * s

    rows_dev = rows_all // size
    at = lax.broadcasted_iota(jnp.int32, (1, rows_all), 1)
    block = at // rows_dev
    rel = ((block & (size // 2 - 1)) << 1) | (block >> (bits - 1))
    offset = ((rel ^ me) & (size // 2 - 1)) * rows_dev + at % rows_dev
    limit = (offset % SPAN).astype(F32)

    def expand(h):
        weights = split(jnp.concatenate([ku_ref[h], vu_ref[h]], axis=1))
        kv = mul(
            stack3((lat_hi[...], lat_lo[...]), 1, False), stack3(weights, 0, True), plain
        )
        hi, lo = split(kv[:, :NOPE])
        key_hi[h] = hi
        key_lo[h] = lo
        hi, lo = split(jnp.transpose(kv[:, NOPE:]))
        val_t[h, :VDIM, :] = hi
        val_t[h, VDIM:, :] = lo

    def compare(h):
        q = stack3(split(q_ref[h]), 1, True)
        hi = jnp.concatenate([key_hi[h], rope_hi[...]], axis=1)
        lo = jnp.concatenate([key_lo[h], rope_lo[...]], axis=1)
        score_ref[h] = mul(stack3((hi, lo), 1, False), q, ((1,), (1,)))

    def weigh(h):
        if last:
            top, total = m_in[h, 0:1, :], l_in[h, 0:1, :]
        else:
            top = jnp.full((1, rows_all), FLOOR, F32)
            total = jnp.zeros((1, rows_all), F32)
        new = top
        for t in range(0, slots, TILE):
            span = slice(t, t + TILE)
            reach = jnp.concatenate([reach_ref[span, :]] * (rows_all // LANES), axis=1)
            score = jnp.where(reach <= limit, score_ref[h, span, :], LOW)
            score_ref[h, span, :] = score
            new = jnp.maximum(new, jnp.max(score, axis=0, keepdims=True))
        fade = jnp.exp(top - new)
        total = total * fade
        for t in range(0, slots, TILE):
            span = slice(t, t + TILE)
            expo = jnp.exp(score_ref[h, span, :] - new)
            total = total + jnp.sum(expo, axis=0, keepdims=True)
            hi, lo = split(expo)
            expo_hi[h, span, :] = hi
            expo_lo[h, span, :] = lo
        return new, total, fade

    def average(h, state):
        top, total, fade = state
        wide = mul(val_t[h], expo_hi[h], plain)
        thin = mul(val_t[h, :VDIM, :], expo_lo[h], plain)
        acc = wide[:VDIM] + (wide[VDIM:] + thin)
        if last:
            acc = acc_in[h] * fade + acc
            hi, lo = split(jnp.transpose(acc / total))
            hi_out[:, h * VDIM : (h + 1) * VDIM] = hi
            lo_out[:, h * VDIM : (h + 1) * VDIM] = lo
        else:
            m_out[h] = jnp.broadcast_to(top, (8, rows_all))
            l_out[h] = jnp.broadcast_to(total, (8, rows_all))
            acc_out[h] = acc

    expand(0)
    compare(0)
    for h in range(PAIR):
        if h + 1 < PAIR:
            expand(h + 1)
        state = weigh(h)
        if h + 1 < PAIR:
            compare(h + 1)
        average(h, state)


def attend(size, me, prefix, count, pieces, places, q, key_up, value_up, state):
    heads, rows_all, _ = q.shape
    slots = sum(p.shape[0] * p.shape[1] for p in pieces)
    last = state is not None
    whole = lambda p: pl.BlockSpec(p.shape, lambda h, *_: (0,) * p.ndim)
    per_head = lambda *shape: pl.BlockSpec((PAIR,) + shape, lambda h, *_: (h, 0, 0))
    column = pl.BlockSpec((rows_all, PAIR * VDIM), lambda h, *_: (0, h))
    in_specs = [whole(count)] + [whole(p) for p in pieces] + [
        per_head(rows_all, 2 * NOPE),
        per_head(LATENT, NOPE),
        per_head(LATENT, VDIM),
    ]
    operands = list(pieces) + [q, key_up, value_up]
    states = [per_head(8, rows_all), per_head(8, rows_all), per_head(VDIM, rows_all)]
    wide = lambda rows: jax.ShapeDtypeStruct((heads, rows, rows_all), F32)
    if last:
        in_specs += states
        operands += list(state)
        half = jax.ShapeDtypeStruct((rows_all, heads * VDIM), BF16)
        out_shape, out_specs = (half, half), (column, column)
    else:
        out_shape, out_specs = (wide(8), wide(8), wide(VDIM)), tuple(states)
    flops = 3 * 2 * heads * slots * (LATENT * 2 * NOPE + rows_all * 3 * NOPE)
    return pl.pallas_call(
        functools.partial(attend_kernel, size, places, last),
        out_shape=out_shape,
        grid_spec=pltpu.PrefetchScalarGridSpec(
            num_scalar_prefetch=2,
            grid=(heads // PAIR,),
            in_specs=in_specs,
            out_specs=out_specs,
            scratch_shapes=[
                pltpu.VMEM((slots, LATENT), BF16),
                pltpu.VMEM((slots, LATENT), BF16),
                pltpu.VMEM((slots, LANES), BF16),
                pltpu.VMEM((slots, LANES), BF16),
                pltpu.VMEM((PAIR, slots, NOPE), BF16),
                pltpu.VMEM((PAIR, slots, NOPE), BF16),
                pltpu.VMEM((PAIR, 2 * VDIM, slots), BF16),
                pltpu.VMEM((slots, LANES), F32),
                pltpu.VMEM((PAIR, slots, rows_all), F32),
                pltpu.VMEM((PAIR, slots, rows_all), BF16),
                pltpu.VMEM((PAIR, slots, rows_all), BF16),
            ],
        ),
        cost_estimate=pl.CostEstimate(
            flops=flops, bytes_accessed=slots * PACKED * 4 + 4 * heads * LATENT * 2 * NOPE, transcendentals=heads * rows_all * slots
        ),
        compiler_params=pltpu.CompilerParams(vmem_limit_bytes=32 * 1024 * 1024),
        name="attend_last" if last else "attend_first",
    )(me, prefix, count, *operands)


def project_kernel(hi_ref, lo_ref, w_ref, keep_ref, send_ref):
    rows = keep_ref.shape[0]
    w_hi, w_lo = split(w_ref[...])
    hi = hi_ref[...]
    mul = lambda x, y: jnp.dot(x, y, preferred_element_type=F32)
    tall = mul(jnp.concatenate([hi, lo_ref[...]], axis=0), w_hi)
    out = tall[: 2 * rows] + (tall[2 * rows :] + mul(hi, w_lo))
    keep_ref[...] = out[:rows]
    send_ref[...] = out[rows:]


def project(hi, lo, out_weight, start, stop):
    rows, depth = hi.shape
    steps = (stop - start) // BLOCK
    first = start // BLOCK
    half = jax.ShapeDtypeStruct((rows // 2, stop - start), F32)
    whole = pl.BlockSpec((rows, depth), lambda i: (0, 0))
    out = pl.BlockSpec((rows // 2, BLOCK), lambda i: (0, i))
    return pl.pallas_call(
        project_kernel,
        out_shape=(half, half),
        grid=(steps,),
        in_specs=[whole, whole, pl.BlockSpec((depth, BLOCK), lambda i: (0, first + i))],
        out_specs=(out, out),
        cost_estimate=pl.CostEstimate(
            flops=6 * rows * depth * (stop - start), bytes_accessed=4 * (depth + rows) * (stop - start), transcendentals=0
        ),
        compiler_params=pltpu.CompilerParams(vmem_limit_bytes=24 * 1024 * 1024),
        name="project",
    )(hi, lo, out_weight)


def spread(taken, extra):
    out = []
    for index in range(1 << len(taken)):
        out.append(sum(((index >> j) & 1) << b for j, b in enumerate(taken)) | extra)
    return out


together = lax.optimization_barrier


def grow(held, bit, size):
    return jnp.concatenate([held, swap(held, bit, size)], axis=0)


def gather(cache, owner, size, orders, q):
    top = size.bit_length() - 2
    slots = cache.shape[0]
    packed, count = pack(cache, owner)
    count = count[None]
    got = swap(packed, top, size)
    steps = list(range(top + 1))
    early = max(len(steps) - 2, 0)
    for bit in steps[:early]:
        count = grow(count, bit, size)
    held = []
    for a, b in cuts(slots, 8):
        held.append(jnp.stack([packed[a:b], got[a:b]]))
    middles = [order[1:-1][::-1] for order in orders]
    done = [[top] for _ in orders]
    late = steps[early:]
    for stage in range(len(middles[0]) - 1):
        *held, count, q = together(tuple(held) + (count, q))
        held = [grow(h, m[stage], size) for h, m in zip(held, middles)]
        done = [d + [m[stage]] for d, m in zip(done, middles)]
        if late:
            count = grow(count, late.pop(0), size)
    *held, count = together(tuple(held) + (count,))
    for bit in late:
        count = grow(count, bit, size)
    far = [swap(h, m[-1], size) for h, m in zip(held, middles)]
    near = [(h, swap(h, 0, size)) for h in held]
    near = [x for pair in near for x in pair]
    near_at = [x for d in done for x in (spread(d, 0), spread(d, 1))]
    far_at = [x for d, m in zip(done, middles) for x in (spread(d, 1 << m[-1]), spread(d, 1 | 1 << m[-1]))]
    return q, count, near, near_at, far, far_at


def project_scatter(hi, lo, out_weight, size, rows_dev, orders):
    bits = size.bit_length() - 1
    shape = (2,) * (bits - 1) + (rows_dev,)
    keeps, sends = [], []
    lefts = [list(range(bits - 1, 0, -1)) for _ in orders]
    spans = cuts(out_weight.shape[1], BLOCK)

    def step(p, stage, got):
        axis = lefts[p].index(orders[p][stage])
        lefts[p].remove(orders[p][stage])
        side = lambda x, b: lax.index_in_dim(x, b, axis, False)
        send = side(keeps[p], 1) + side(got, 1)
        keeps[p] = (side(keeps[p], 0), side(got, 0))
        return send

    def hop(p, stage):
        return swap(sends[p], orders[p][stage], size)

    flights = []
    for p, (a, b) in enumerate(spans):
        if p >= 2:
            sends[p - 2] = step(p - 2, 1, flights[p - 2])
            flights[p - 2] = hop(p - 2, 1)
        keep, send = project(hi, lo, out_weight, a, b)
        keeps.append(keep.reshape(shape + (b - a,)))
        sends.append(send.reshape(shape + (b - a,)))
        flights.append(hop(p, 0))
    for p in range(max(len(spans) - 2, 0), len(spans)):
        sends[p] = step(p, 1, flights[p])
        flights[p] = hop(p, 1)
    for stage in range(2, bits + 1):
        kept = [k[0] for k in keeps]
        out = together(tuple(kept) + tuple(sends))
        keeps = [o + k[1] for o, k in zip(out, keeps)]
        for p in range(len(spans)):
            if stage == bits:
                keeps[p] = keeps[p] + flights[p]
            else:
                sends[p] = step(p, stage, flights[p])
                flights[p] = hop(p, stage)
    return jnp.concatenate(keeps, axis=1)


def on_device(size, queries, cache, owner, prefix_len, key_up, value_up, out_weight):
    bits = size.bit_length() - 1
    heads = key_up.shape[0]
    rows_dev = queries.shape[0] // size
    me = lax.axis_index("blk")
    orders = orders_of(bits)
    me_arg = me.reshape(1).astype(jnp.int32)
    q = arrange(size, me_arg, queries, heads)
    q, count, near, near_at, far, far_at = gather(cache, owner, size, orders, q)
    state = attend(size, me_arg, prefix_len, count, near, near_at, q, key_up, value_up, None)
    *far, a, b, c = together(tuple(far) + tuple(state))
    far = [x for f in far for x in (f, swap(f, 0, size))]
    hi, lo = attend(size, me_arg, prefix_len, count, far, far_at, q, key_up, value_up, (a, b, c))
    return project_scatter(hi, lo, out_weight, size, rows_dev, orders)


def solution(mesh):
    placed = (
        P("groups", "blk"),
        P(("groups", "blk"), None),
        P(("groups", "blk")),
        P("groups"),
        P("blk", None, None),
        P("blk", None, None),
        P("blk", None),
    )
    size = mesh.shape["blk"]

    def step(*args):
        return on_device(size, *args)

    return jax.shard_map(
        step, mesh=mesh, in_specs=placed, out_specs=P(("groups", "blk"), None), check_vma=False
    )
```

```python
import functools
import math

import jax
import jax.numpy as jnp
from jax import lax
from jax.experimental import pallas as pl
from jax.experimental.pallas import tpu as pltpu
from jax.sharding import PartitionSpec as P


LATENT = 512
ROPE = 64
NOPE = 128
VDIM = 128
SPAN = 128
REQS = 2
PARTS = 3
LANES = 128
PACKED = LATENT + LANES
BLOCK = 512
FAR = 1e9
LOW = -1e30
FLOOR = -1e29
TILE = 256
PAIR = 2
CHUNKS = 4
F32 = jnp.float32
BF16 = jnp.bfloat16


def orders_of(bits):
    middle = list(range(1, bits - 1))
    out = []
    for p in range(PARTS):
        turn = p % max(len(middle), 1)
        out.append([0] + middle[turn:] + middle[:turn] + [bits - 1])
    return out


def cuts(total, unit):
    units = total // unit
    edges = [-(-units * p // PARTS) * unit for p in range(PARTS)] + [total]
    return [(edges[p], edges[p + 1]) for p in range(PARTS)]


def swap(x, bit, size):
    return lax.ppermute(x, "blk", [(i, i ^ (1 << bit)) for i in range(size)])


def split(x):
    hi = x.astype(BF16)
    return hi, (x - hi.astype(F32)).astype(BF16)


def pack_kernel(cache_ref, owner_ref, out_ref, count_ref):
    slots = cache_ref.shape[0]
    row = lax.broadcasted_iota(jnp.int32, (slots, slots), 0)
    col = lax.broadcasted_iota(jnp.int32, (slots, slots), 1)
    who = jnp.broadcast_to(owner_ref[...].astype(F32), (slots, slots))
    mine = jnp.sum(jnp.where(row == col, who, 0.0), axis=1, keepdims=True)
    ones = jnp.sum(jnp.where(col < row, who, 0.0), axis=1, keepdims=True)
    place = lax.broadcasted_iota(jnp.int32, (slots, 1), 0).astype(F32)
    rank = jnp.where(mine == 1.0, ones, place - ones)
    out_ref[:, :LATENT] = cache_ref[:, :LATENT]
    out_ref[:, LATENT : LATENT + ROPE] = cache_ref[:, LATENT:]
    lane = lax.broadcasted_iota(jnp.int32, (slots, LANES - ROPE), 1)
    out_ref[:, LATENT + ROPE :] = jnp.where(lane == 0, mine, jnp.where(lane == 1, rank, 0.0))
    total = jnp.sum(owner_ref[...].astype(F32), axis=1, keepdims=True)
    which = lax.broadcasted_iota(jnp.int32, count_ref.shape, 0)
    count_ref[...] = jnp.where(which == 0, slots - total, total)


def pack(cache, owner):
    slots = cache.shape[0]
    return pl.pallas_call(
        pack_kernel,
        out_shape=(
            jax.ShapeDtypeStruct((slots, PACKED), F32),
            jax.ShapeDtypeStruct((8, LANES), F32),
        ),
        name="pack",
    )(cache, owner.reshape(1, slots))


def query_kernel(size, me_ref, q_ref, out_ref):
    heads = out_ref.shape[0]
    rows_dev = q_ref.shape[1]
    bits = size.bit_length() - 1
    width = NOPE + ROPE
    blank = jnp.zeros((rows_dev, 2 * NOPE - width), F32)
    for place in range(size):
        rel = ((place & (size // 2 - 1)) << 1) | (place >> (bits - 1))
        x = q_ref[rel ^ me_ref[0]] * (1.0 / math.sqrt(width))
        rows = slice(place * rows_dev, (place + 1) * rows_dev)
        for h in range(heads):
            at = h * width
            out_ref[h, rows, :NOPE] = x[:, at : at + NOPE]
            out_ref[h, rows, NOPE:] = jnp.concatenate([x[:, at + NOPE : at + width], blank], axis=1)


def arrange(size, me, queries, heads):
    rows_all, cols = queries.shape
    return pl.pallas_call(
        functools.partial(query_kernel, size),
        out_shape=jax.ShapeDtypeStruct((heads, rows_all, 2 * NOPE), F32),
        grid_spec=pltpu.PrefetchScalarGridSpec(
            num_scalar_prefetch=1,
            grid=(1,),
            in_specs=[pl.BlockSpec((size, rows_all // size, cols), lambda i, *_: (0, 0, 0))],
            out_specs=pl.BlockSpec((heads, rows_all, 2 * NOPE), lambda i, *_: (0, 0, 0)),
        ),
        cost_estimate=pl.CostEstimate(flops=0, bytes_accessed=8 * rows_all * cols, transcendentals=0),
        name="arrange",
    )(me, queries.reshape(size, rows_all // size, cols))


def stack3(x, axis, low):
    hi, lo = x
    return jnp.concatenate([hi, lo, hi] if low else [hi, hi, lo], axis=axis)


def attend_kernel(size, places, last, me_ref, prefix_ref, count_ref, *refs):
    n = 2 * PARTS
    pieces = refs[:n]
    q_ref, ku_ref, vu_ref = refs[n : n + 3]
    refs = refs[n + 3 :]
    if last:
        m_in, l_in, acc_in, hi_out, lo_out = refs[:5]
        refs = refs[5:]
    else:
        m_out, l_out, acc_out = refs[:3]
        refs = refs[3:]
    lat_hi, lat_lo, rope_hi, rope_lo, key_hi, key_lo, val_t, reach_ref, score_ref, expo_hi, expo_lo = refs
    rows_all = q_ref.shape[1]
    slots = lat_hi.shape[0]
    me = me_ref[0]
    bits = size.bit_length() - 1
    mul = lambda x, y, c: lax.dot_general(x, y, (c, ((), ())), preferred_element_type=F32)
    plain = ((1,), (0,))
    half = LANES // REQS

    @pl.when(pl.program_id(0) == 0)
    def _():
        at = 0
        for ref in pieces:
            m, s, _ = ref.shape
            for j in range(0, m, 2):
                x = ref[j : j + 2].reshape(2 * s, PACKED)
                hi, lo = split(x)
                rows = slice(at + j * s, at + (j + 2) * s)
                lat_hi[rows, :] = hi[:, :LATENT]
                lat_lo[rows, :] = lo[:, :LATENT]
                rope_hi[rows, :] = hi[:, LATENT:]
                rope_lo[rows, :] = lo[:, LATENT:]
            at += m * s
        row = lax.broadcasted_iota(jnp.int32, (LANES, 2 * LANES), 0)
        col = lax.broadcasted_iota(jnp.int32, (LANES, 2 * LANES), 1)
        pick = jnp.where(row == ROPE + col // LANES, 1.0, 0.0).astype(BF16)
        told = mul(rope_hi[...], pick, plain)
        lane = lax.broadcasted_iota(jnp.int32, (1, LANES), 1)
        want = ((lane // half) ^ (me >> (bits - 1))).astype(F32)
        index = lax.broadcasted_iota(jnp.int32, (size, LANES), 0)
        device = index ^ me
        counts = jnp.where(want == 0.0, count_ref[:, 0, :], count_ref[:, 1, :])
        ahead = jnp.where(want == 0.0, prefix_ref[0].astype(F32), prefix_ref[1].astype(F32))
        at = 0
        for ref, where in zip(pieces, places):
            m, s, _ = ref.shape
            for j, r in enumerate(where):
                before = jnp.where(device < (me ^ r), counts, 0.0)
                base = jnp.sum(before, axis=0, keepdims=True) - ahead
                rows = slice(at + j * s, at + (j + 1) * s)
                here = told[rows, LANES:] + base
                reach_ref[rows, :] = jnp.where(told[rows, :LANES] == want, here, FAR)
            at += m * s

    rows_dev = rows_all // size
    at = lax.broadcasted_iota(jnp.int32, (1, rows_all), 1)
    block = at // rows_dev
    rel = ((block & (size // 2 - 1)) << 1) | (block >> (bits - 1))
    offset = ((rel ^ me) & (size // 2 - 1)) * rows_dev + at % rows_dev
    limit = (offset % SPAN).astype(F32)

    chunk = slots // CHUNKS

    def expand(h, c):
        rows = slice(c * chunk, (c + 1) * chunk)
        weights = split(jnp.concatenate([ku_ref[h], vu_ref[h]], axis=1))
        kv = mul(
            stack3((lat_hi[rows, :], lat_lo[rows, :]), 1, False), stack3(weights, 0, True), plain
        )
        hi, lo = split(kv[:, :NOPE])
        key_hi[h, rows, :] = hi
        key_lo[h, rows, :] = lo
        hi, lo = split(jnp.transpose(kv[:, NOPE:]))
        val_t[h, :VDIM, rows] = hi
        val_t[h, VDIM:, rows] = lo

    def compare(h):
        q = stack3(split(q_ref[h]), 1, True)
        hi = jnp.concatenate([key_hi[h], rope_hi[...]], axis=1)
        lo = jnp.concatenate([key_lo[h], rope_lo[...]], axis=1)
        score_ref[h] = mul(stack3((hi, lo), 1, False), q, ((1,), (1,)))

    def weigh(h, between):
        if last:
            top, total = m_in[h, 0:1, :], l_in[h, 0:1, :]
        else:
            top = jnp.full((1, rows_all), FLOOR, F32)
            total = jnp.zeros((1, rows_all), F32)
        new = top
        turns = slots // TILE
        between = [between[i * len(between) // (2 * turns) : (i + 1) * len(between) // (2 * turns)] for i in range(2 * turns)]
        for t in range(0, slots, TILE):
            for run in between.pop(0):
                run()
            span = slice(t, t + TILE)
            reach = jnp.concatenate([reach_ref[span, :]] * (rows_all // LANES), axis=1)
            score = jnp.where(reach <= limit, score_ref[h, span, :], LOW)
            score_ref[h, span, :] = score
            new = jnp.maximum(new, jnp.max(score, axis=0, keepdims=True))
        fade = jnp.exp(top - new)
        total = total * fade
        for t in range(0, slots, TILE):
            for run in between.pop(0):
                run()
            span = slice(t, t + TILE)
            expo = jnp.exp(score_ref[h, span, :] - new)
            total = total + jnp.sum(expo, axis=0, keepdims=True)
            hi, lo = split(expo)
            expo_hi[h, span, :] = hi
            expo_lo[h, span, :] = lo
        return new, total, fade

    def average(h, state):
        top, total, fade = state
        wide = mul(val_t[h], expo_hi[h], plain)
        thin = mul(val_t[h, :VDIM, :], expo_lo[h], plain)
        acc = wide[:VDIM] + (wide[VDIM:] + thin)
        if last:
            acc = acc_in[h] * fade + acc
            hi, lo = split(jnp.transpose(acc / total))
            hi_out[:, h * VDIM : (h + 1) * VDIM] = hi
            lo_out[:, h * VDIM : (h + 1) * VDIM] = lo
        else:
            m_out[h] = jnp.broadcast_to(top, (8, rows_all))
            l_out[h] = jnp.broadcast_to(total, (8, rows_all))
            acc_out[h] = acc

    for c in range(CHUNKS):
        expand(0, c)
    compare(0)
    for h in range(PAIR):
        more = [functools.partial(expand, h + 1, c) for c in range(CHUNKS)] if h + 1 < PAIR else []
        state = weigh(h, more)
        if h + 1 < PAIR:
            compare(h + 1)
        average(h, state)


def attend(size, me, prefix, count, pieces, places, q, key_up, value_up, state):
    heads, rows_all, _ = q.shape
    slots = sum(p.shape[0] * p.shape[1] for p in pieces)
    last = state is not None
    whole = lambda p: pl.BlockSpec(p.shape, lambda h, *_: (0,) * p.ndim)
    per_head = lambda *shape: pl.BlockSpec((PAIR,) + shape, lambda h, *_: (h, 0, 0))
    column = pl.BlockSpec((rows_all, PAIR * VDIM), lambda h, *_: (0, h))
    in_specs = [whole(count)] + [whole(p) for p in pieces] + [
        per_head(rows_all, 2 * NOPE),
        per_head(LATENT, NOPE),
        per_head(LATENT, VDIM),
    ]
    operands = list(pieces) + [q, key_up, value_up]
    states = [per_head(8, rows_all), per_head(8, rows_all), per_head(VDIM, rows_all)]
    wide = lambda rows: jax.ShapeDtypeStruct((heads, rows, rows_all), F32)
    if last:
        in_specs += states
        operands += list(state)
        half = jax.ShapeDtypeStruct((rows_all, heads * VDIM), BF16)
        out_shape, out_specs = (half, half), (column, column)
    else:
        out_shape, out_specs = (wide(8), wide(8), wide(VDIM)), tuple(states)
    flops = 3 * 2 * heads * slots * (LATENT * 2 * NOPE + rows_all * 3 * NOPE)
    return pl.pallas_call(
        functools.partial(attend_kernel, size, places, last),
        out_shape=out_shape,
        grid_spec=pltpu.PrefetchScalarGridSpec(
            num_scalar_prefetch=2,
            grid=(heads // PAIR,),
            in_specs=in_specs,
            out_specs=out_specs,
            scratch_shapes=[
                pltpu.VMEM((slots, LATENT), BF16),
                pltpu.VMEM((slots, LATENT), BF16),
                pltpu.VMEM((slots, LANES), BF16),
                pltpu.VMEM((slots, LANES), BF16),
                pltpu.VMEM((PAIR, slots, NOPE), BF16),
                pltpu.VMEM((PAIR, slots, NOPE), BF16),
                pltpu.VMEM((PAIR, 2 * VDIM, slots), BF16),
                pltpu.VMEM((slots, LANES), F32),
                pltpu.VMEM((PAIR, slots, rows_all), F32),
                pltpu.VMEM((PAIR, slots, rows_all), BF16),
                pltpu.VMEM((PAIR, slots, rows_all), BF16),
            ],
        ),
        cost_estimate=pl.CostEstimate(
            flops=flops, bytes_accessed=slots * PACKED * 4 + 4 * heads * LATENT * 2 * NOPE, transcendentals=heads * rows_all * slots
        ),
        compiler_params=pltpu.CompilerParams(vmem_limit_bytes=32 * 1024 * 1024),
        name="attend_last" if last else "attend_first",
    )(me, prefix, count, *operands)


def project_kernel(start, hi_ref, lo_ref, w_ref, keep_ref, send_ref):
    rows, cols = keep_ref.shape
    hi = hi_ref[...]
    both = jnp.concatenate([hi, lo_ref[...]], axis=0)
    mul = lambda x, y: jnp.dot(x, y, preferred_element_type=F32)
    for c in range(0, cols, TILE):
        w_hi, w_lo = split(w_ref[:, start + c : start + c + TILE])
        tall = mul(both, w_hi)
        out = tall[: 2 * rows] + (tall[2 * rows :] + mul(hi, w_lo))
        keep_ref[:, c : c + TILE] = out[:rows]
        send_ref[:, c : c + TILE] = out[rows:]


def project(hi, lo, out_weight, start, stop):
    rows, depth = hi.shape
    half = jax.ShapeDtypeStruct((rows // 2, stop - start), F32)
    vmem = pl.BlockSpec(memory_space=pltpu.VMEM)
    return pl.pallas_call(
        functools.partial(project_kernel, start),
        out_shape=(half, half),
        in_specs=[vmem, vmem, vmem],
        out_specs=(vmem, vmem),
        cost_estimate=pl.CostEstimate(
            flops=6 * rows * depth * (stop - start), bytes_accessed=4 * (depth + rows) * (stop - start), transcendentals=0
        ),
        compiler_params=pltpu.CompilerParams(vmem_limit_bytes=30 * 1024 * 1024),
        name="project",
    )(hi, lo, out_weight)


def spread(taken, extra):
    out = []
    for index in range(1 << len(taken)):
        out.append(sum(((index >> j) & 1) << b for j, b in enumerate(taken)) | extra)
    return out


together = lax.optimization_barrier


def grow(held, bit, size):
    return jnp.concatenate([held, swap(held, bit, size)], axis=0)


def gather(cache, owner, size, orders, q):
    top = size.bit_length() - 2
    slots = cache.shape[0]
    packed, count = pack(cache, owner)
    count = count[None]
    got = swap(packed, top, size)
    steps = list(range(top + 1))
    early = max(len(steps) - 2, 0)
    for bit in steps[:early]:
        count = grow(count, bit, size)
    held = []
    for a, b in cuts(slots, 8):
        held.append(jnp.stack([packed[a:b], got[a:b]]))
    middles = [order[1:-1][::-1] for order in orders]
    done = [[top] for _ in orders]
    late = steps[early:]
    for stage in range(len(middles[0]) - 1):
        if stage == len(middles[0]) - 2:
            *held, count, q = together(tuple(held) + (count, q))
        else:
            *held, count = together(tuple(held) + (count,))
        for p, m in enumerate(middles):
            held[p] = grow(held[p], m[stage], size)
        done = [d + [m[stage]] for d, m in zip(done, middles)]
        if late:
            count = grow(count, late.pop(0), size)
    *held, count = together(tuple(held) + (count,))
    for bit in late:
        count = grow(count, bit, size)
    far = [swap(h, m[-1], size) for h, m in zip(held, middles)]
    near = [(h, swap(h, 0, size)) for h in held]
    near = [x for pair in near for x in pair]
    near_at = [x for d in done for x in (spread(d, 0), spread(d, 1))]
    far_at = [x for d, m in zip(done, middles) for x in (spread(d, 1 << m[-1]), spread(d, 1 | 1 << m[-1]))]
    return q, count, near, near_at, far, far_at


def project_scatter(hi, lo, out_weight, size, rows_dev, orders):
    bits = size.bit_length() - 1
    shape = (2,) * (bits - 1) + (rows_dev,)
    keeps, sends = [], []
    lefts = [list(range(bits - 1, 0, -1)) for _ in orders]
    spans = cuts(out_weight.shape[1], BLOCK)

    def step(p, stage, got):
        axis = lefts[p].index(orders[p][stage])
        lefts[p].remove(orders[p][stage])
        side = lambda x, b: lax.index_in_dim(x, b, axis, False)
        send = side(keeps[p], 1) + side(got, 1)
        keeps[p] = (side(keeps[p], 0), side(got, 0))
        return send

    def hop(p, stage):
        return swap(sends[p], orders[p][stage], size)

    flights = []
    for p, (a, b) in enumerate(spans):
        if p >= 2:
            sends[p - 2] = step(p - 2, 1, flights[p - 2])
            flights[p - 2] = hop(p - 2, 1)
        keep, send = project(hi, lo, out_weight, a, b)
        keeps.append(keep.reshape(shape + (b - a,)))
        sends.append(send.reshape(shape + (b - a,)))
        flights.append(hop(p, 0))
    for p in range(max(len(spans) - 2, 0), len(spans)):
        sends[p] = step(p, 1, flights[p])
        flights[p] = hop(p, 1)
    for stage in range(2, bits + 1):
        kept = [k[0] for k in keeps]
        out = together(tuple(kept) + tuple(sends))
        keeps = [o + k[1] for o, k in zip(out, keeps)]
        for p in range(len(spans)):
            if stage == bits:
                keeps[p] = keeps[p] + flights[p]
            else:
                sends[p] = step(p, stage, flights[p])
                flights[p] = hop(p, stage)
    return jnp.concatenate(keeps, axis=1)


def on_device(size, queries, cache, owner, prefix_len, key_up, value_up, out_weight):
    bits = size.bit_length() - 1
    heads = key_up.shape[0]
    rows_dev = queries.shape[0] // size
    me = lax.axis_index("blk")
    orders = orders_of(bits)
    me_arg = me.reshape(1).astype(jnp.int32)
    q = arrange(size, me_arg, queries, heads)
    q, count, near, near_at, far, far_at = gather(cache, owner, size, orders, q)
    state = attend(size, me_arg, prefix_len, count, near, near_at, q, key_up, value_up, None)
    *far, a, b, c = together(tuple(far) + tuple(state))
    far = [x for f in far for x in (f, swap(f, 0, size))]
    hi, lo = attend(size, me_arg, prefix_len, count, far, far_at, q, key_up, value_up, (a, b, c))
    return project_scatter(hi, lo, out_weight, size, rows_dev, orders)


def solution(mesh):
    placed = (
        P("groups", "blk"),
        P(("groups", "blk"), None),
        P(("groups", "blk")),
        P("groups"),
        P("blk", None, None),
        P("blk", None, None),
        P("blk", None),
    )
    size = mesh.shape["blk"]

    def step(*args):
        return on_device(size, *args)

    return jax.shard_map(
        step, mesh=mesh, in_specs=placed, out_specs=P(("groups", "blk"), None), check_vma=False
    )
```
